32 devices in a mesh: groups: 2 (over y), ctx: 4 (over z), exp: 2 (over x), head: 2 (over core).
Axes of the slice: x: 2, y: 2, z: 4, core: 2. Of those that a mesh axis runs over, the one named last changes fastest.
Arguments:
- latent: bfloat16 [256, 576], P(('groups', 'ctx')), parts along dimension 0, may hold values from -5 to 5
- query: bfloat16 [256, 3072], P(('groups', 'ctx'), ('exp', 'head')), parts along dimension 0, may hold values from -30 to 30
- w_uk: bfloat16 [512, 2048], P(None, ('exp', 'head')), may hold values from -0.25 to 0.25
- w_uv: bfloat16 [512, 2048], P(None, ('exp', 'head')), may hold values from -0.25 to 0.25
- w_o: bfloat16 [2048, 3584], P(('exp', 'head'), 'ctx'), may hold values from -0.5 to 0.5
- resid: bfloat16 [256, 3584], P(('groups', 'ctx', 'exp', 'head')), parts along dimension 0, may hold values from -6 to 6
- norm_gain: float32 [3584], replicated, may hold values from 0.1 to 1.9
- w_gate: bfloat16 [4, 3584, 2048], P(('exp', 'head'), None, 'ctx'), may hold values from -0.09375 to 0.09375
- w_up: bfloat16 [4, 3584, 2048], P(('exp', 'head'), None, 'ctx'), may hold values from -0.09375 to 0.09375
- w_down: bfloat16 [4, 2048, 3584], P(('exp', 'head'), None, 'ctx'), may hold values from -0.125 to 0.125
- expert_ids: int32 [256, 2], P(('groups', 'ctx', 'exp', 'head')), parts along dimension 0, may hold values from 0 to 3, all different within a row; in each aligned block of 8 rows (0 to 7, 8 to 15, ...) at most 8 rows name the same one
- route_weights: float32 [256, 2], P(('groups', 'ctx', 'exp', 'head')), parts along dimension 0, may hold values from 0.2 to 1
Outputs:
- layer_out: bfloat16 [256, 3584], P(('groups', 'ctx', 'exp', 'head')), parts along dimension 0
The draws below stay inside these ranges and needn't reach their ends.
There are 2 independent parts, one for each index of `groups`. The reference program is written for one: setup_inputs(seed, part) draws one part's arguments, and reference() takes and returns one part's arrays. A program takes and returns all parts, laid end to end along the dimension named above; an argument that names none is the same for every part. Nothing has to cross between parts.
Inputs may be any that keep to these rules, and one draw needn't show every extreme that they name: `expert_ids`: each token names 2 different experts; within each aligned block of 8 tokens no expert is named more than 8 times, a bound that some block reaches.
All inputs are finite; a program needn't handle non-finite values.
Results may differ from the reference program's by a relative error of at most 0.014.
Values may be sent and summed in bfloat16 or wider, within the bound.
A program may use at most 64 MiB of HBM per device.

```python
import math
import jax
import jax.numpy as jnp
import numpy as np
from jax import lax

D = 3584
NOPE = 128
ROPE = 64
LATENT = 512
HEAD_DEV = 4
MOE_FF = 2048
TOP = 2
TOK_DEV = 8
SEQ = 128
HEADS = 16
EXPERTS = 4
CAP = 8


def draw_latent(key, part):
    base_key = jax.random.fold_in(key, 11)
    values = jnp.clip(jax.random.normal(base_key, (SEQ, LATENT + ROPE), jnp.float32), -5.0, 5.0)
    return values.astype(jnp.bfloat16)


def draw_query(key, part):
    base_key = jax.random.fold_in(key, 13)
    head_width = NOPE + ROPE
    values = jnp.clip(jax.random.normal(base_key, (SEQ, HEADS, head_width), jnp.float32), -5.0, 5.0)
    return values.reshape(SEQ, HEADS * head_width).astype(jnp.bfloat16)


def block_scale(own_key, extent, cuts, low, top_value):
    def one(position, shards_of):
        heights = jax.random.uniform(jax.random.fold_in(jax.random.fold_in(own_key, 6), position), (shards_of,), jnp.float32, low / len(cuts), top_value / len(cuts))
        return jnp.repeat(jnp.exp(heights), extent[position] // shards_of).reshape((-1,) + (1,) * (len(extent) - position - 1))

    level = one(*cuts[0])
    for cut in cuts[1:]:
        level = level * one(*cut)
    return level


def assign_block(key, own, number, rows, count, top, reach, lean):
    ranking = jax.random.permutation(key, count)
    crowded, usual = load_shares(count, rows * top, reach, lean, True), load_shares(count, rows * top, reach, lean, False)
    places = jnp.arange(count)

    def named(tallies, turn):
        used = int((tallies > 0).sum())
        fixed = max(1, used // 4)
        passed = fixed + (places - fixed + turn * (used - fixed)) % max(1, count - fixed)
        return jnp.zeros((count,), jnp.int32).at[ranking[jnp.where(places < fixed, places, passed)]].set(jnp.asarray(tallies, jnp.int32))

    tallies = jnp.where(number % 4 == 0, named(crowded, number // 4), named(usual, number - number // 4 - 1))
    mixed = jax.random.permutation(jax.random.fold_in(own, 3), count)
    giver, taker = mixed[0:count // 2 * 2:2], mixed[1:count // 2 * 2:2]
    slack = jnp.minimum(tallies[giver] - 1, reach - tallies[taker]) // 2
    slack = jnp.where((giver == ranking[0]) | (taker == ranking[0]) | (tallies[taker] == 0), 0, jnp.maximum(slack, 0))
    passed = jax.random.randint(jax.random.fold_in(own, 4), (count // 2,), 0, 1 << 20) % (slack + 1)
    tallies = tallies.at[giver].add(-passed).at[taker].add(passed)
    members = jnp.searchsorted(jnp.cumsum(tallies), jnp.arange(rows * top), side="right").astype(jnp.int32)
    table = members.reshape(top, rows).T
    table = table[jax.random.permutation(jax.random.fold_in(own, 1), rows)]
    turn = jax.random.randint(jax.random.fold_in(own, 2), (rows, 1), 0, top)
    return jnp.take_along_axis(table, (jnp.arange(top)[None, :] + turn) % top, axis=1)


def load_shares(amount, total, limit, lean, full):
    loads = [(1 << 20) // math.isqrt(rank ** lean) + 1 for rank in range(1, amount + 1)]
    largest = limit if full else min(limit, max(-(-total // amount), total * loads[0] // sum(loads)))
    least = 1 if total - largest >= amount - 1 else 0
    given, surplus = [largest] + [least] * (amount - 1), total - largest - least * (amount - 1)
    while surplus > 0:
        candidates = [i for i in range(1, amount) if given[i] < largest] or [i for i in range(1, amount) if given[i] < limit]
        whole, budget = sum([loads[i] for i in candidates]), surplus
        for i in candidates:
            addition = min(limit - given[i], max(1, budget * loads[i] // whole), surplus)
            given[i] = given[i] + addition
            surplus = surplus - addition
    return np.array(given)


def centred(own_key, extent, spread, most, shards=(), kind=jnp.bfloat16):
    result = spread * jax.random.normal(own_key, extent, jnp.float32)
    if shards:
        result = result * block_scale(own_key, extent, shards, -0.22, 0.18)
    return jnp.clip(result, -most, most).astype(kind)


def setup_inputs(seed: int = 0, part: int = 0) -> dict:
    arg_keys = jax.random.split(jax.random.key(seed), 13)
    own_keys = jax.random.split(jax.random.fold_in(arg_keys[12], part), 13)
    latent = draw_latent(jax.random.fold_in(jax.random.fold_in(arg_keys[12], part), 71), part)
    query = draw_query(jax.random.fold_in(jax.random.fold_in(arg_keys[12], part), 71), part)
    w_uk = centred(arg_keys[2], (LATENT, HEADS * NOPE), LATENT ** -0.5, 0.25, ((1, 4),))
    w_uv = centred(arg_keys[3], (LATENT, HEADS * NOPE), LATENT ** -0.5, 0.25, ((1, 4),))
    w_o = centred(arg_keys[4], (HEADS * NOPE, D), (HEADS * NOPE // 16) ** -0.5, 0.5, ((0, 4), (1, 4)))
    resid = centred(own_keys[5], (SEQ, D), 1.0, 6.0, ((0, 16),))
    norm_gain = jnp.clip(1.0 + 0.18 * jax.random.normal(arg_keys[6], (D,), jnp.float32), 0.1, 1.9)
    w_gate = centred(arg_keys[7], (EXPERTS, D, MOE_FF), D ** -0.5, 0.09375, ((0, 4), (2, 4)))
    w_up = centred(arg_keys[8], (EXPERTS, D, MOE_FF), D ** -0.5, 0.09375, ((0, 4), (2, 4)))
    w_down = centred(arg_keys[9], (EXPERTS, MOE_FF, D), MOE_FF ** -0.5, 0.125, ((0, 4), (2, 4)))
    expert_ids_keys = jax.random.split(jax.random.fold_in(own_keys[10], 1), SEQ // TOK_DEV)
    expert_ids_turns = jax.random.permutation(jax.random.fold_in(own_keys[10], 3), SEQ // TOK_DEV)
    expert_ids = jax.vmap(lambda own, number: assign_block(jax.random.fold_in(own_keys[10], 2), own, number, TOK_DEV, EXPERTS, TOP, CAP, 2))(expert_ids_keys, expert_ids_turns).reshape((SEQ, TOP))
    route_weights = jnp.clip(0.2 + 0.8 * jax.random.uniform(own_keys[11], (SEQ, TOP), jnp.float32) ** block_scale(own_keys[11], (SEQ, TOP), ((0, 16),), -0.2, 0.2), 0.2, 1.0)
    return dict(latent=latent, query=query, w_uk=w_uk, w_uv=w_uv, w_o=w_o, resid=resid, norm_gain=norm_gain, w_gate=w_gate, w_up=w_up, w_down=w_down, expert_ids=expert_ids, route_weights=route_weights)


def reference(latent, query, w_uk, w_uv, w_o, resid, norm_gain, w_gate, w_up, w_down, expert_ids, route_weights):
    compressed = latent[:, :LATENT]
    rope_keys = latent[:, LATENT:]
    head_width = NOPE + ROPE
    score_scale = 1.0 / math.sqrt(head_width)
    positions = jnp.arange(SEQ, dtype=jnp.int32)
    allowed = positions[None, :] <= positions[:, None]

    def one_head(unpack):
        query_head, key_proj, value_proj = unpack
        keys_nope = jnp.dot(compressed, key_proj, preferred_element_type=jnp.float32).astype(jnp.bfloat16)
        values_up = jnp.dot(compressed, value_proj, preferred_element_type=jnp.float32).astype(jnp.bfloat16)
        scores = jnp.dot(query_head[:, :NOPE], keys_nope.T, preferred_element_type=jnp.float32)
        scores = (scores + jnp.dot(query_head[:, NOPE:], rope_keys.T, preferred_element_type=jnp.float32)) * score_scale
        largest = lax.optimization_barrier(jnp.max(jnp.where(allowed, scores, -1e+30), axis=1, keepdims=True))
        exponent = jnp.where(allowed, jnp.exp(scores - largest), 0.0)
        probs = exponent.astype(jnp.bfloat16)
        summed = jnp.dot(probs, values_up, preferred_element_type=jnp.float32)
        return (summed / lax.optimization_barrier(jnp.sum(exponent, axis=1, keepdims=True))).astype(jnp.bfloat16)
    query_heads = query.reshape(SEQ, HEADS, head_width).transpose(1, 0, 2)
    key_heads = w_uk.reshape(LATENT, HEADS, NOPE).transpose(1, 0, 2)
    value_heads = w_uv.reshape(LATENT, HEADS, NOPE).transpose(1, 0, 2)
    per_head = lax.map(one_head, (query_heads, key_heads, value_heads))
    attended = per_head.transpose(1, 0, 2).reshape(SEQ, HEADS * NOPE)
    group_count = HEADS // HEAD_DEV
    group_width = HEAD_DEV * NOPE
    attended_groups = attended.reshape(SEQ, group_count, group_width).transpose(1, 0, 2)
    weight_groups = w_o.reshape(group_count, group_width, D)

    def add_group(total, unpack):
        rows, weights = unpack
        head_part = jnp.dot(rows, weights, preferred_element_type=jnp.float32).astype(jnp.bfloat16)
        head_part = lax.optimization_barrier(head_part)
        return (total + head_part.astype(jnp.float32), None)
    projected, unused = lax.scan(add_group, jnp.zeros((SEQ, D), jnp.float32), (attended_groups, weight_groups))
    residual_sum = resid.astype(jnp.float32) + projected
    inverse_rms = lax.rsqrt(lax.optimization_barrier(jnp.mean(residual_sum * residual_sum, axis=1, keepdims=True)) + 1e-06)
    normalized = (residual_sum * inverse_rms * norm_gain).astype(jnp.bfloat16)
    blocks = SEQ // TOK_DEV
    route_count = TOK_DEV * TOP
    block_ids = expert_ids.reshape(blocks, route_count)
    onehot = (block_ids[:, :, None] == jnp.arange(EXPERTS, dtype=jnp.int32)[None, None, :]).astype(jnp.int32)
    slot_rank = lax.optimization_barrier(jnp.sum((jnp.cumsum(onehot, axis=1) - onehot) * onehot, axis=2)).astype(jnp.int32)
    block_index = jnp.arange(blocks, dtype=jnp.int32)[:, None]
    token_index = (block_index * TOK_DEV + jnp.arange(route_count, dtype=jnp.int32)[None, :] // TOP).astype(jnp.int32)
    slot_table = jnp.full((blocks, EXPERTS, CAP), SEQ, jnp.int32)
    slot_table = slot_table.at[jnp.broadcast_to(block_index, (blocks, route_count)), block_ids, slot_rank].set(token_index)
    padded = jnp.concatenate([normalized, jnp.zeros((1, D), normalized.dtype)], axis=0)

    def one_expert(unpack):
        row_ids, gate_proj, up_proj, down_proj = unpack
        inputs = padded[row_ids]
        gate_part = jnp.dot(inputs, gate_proj, preferred_element_type=jnp.float32)
        up_part = jnp.dot(inputs, up_proj, preferred_element_type=jnp.float32)
        expert_hidden = (jax.nn.silu(gate_part) * up_part).astype(jnp.bfloat16)
        return jnp.dot(expert_hidden, down_proj, preferred_element_type=jnp.float32).astype(jnp.bfloat16)
    expert_rows = slot_table.transpose(1, 0, 2).reshape(EXPERTS, blocks * CAP)
    expert_out = lax.map(one_expert, (expert_rows, w_gate, w_up, w_down))
    flat_out = expert_out.reshape(EXPERTS * blocks * CAP, D)
    locate = (block_ids * (blocks * CAP) + block_index * CAP + slot_rank).reshape(SEQ, TOP).astype(jnp.int32)
    picked = flat_out[locate].astype(jnp.float32)
    moe_sum = lax.optimization_barrier(jnp.sum(route_weights[:, :, None] * picked, axis=1))
    return (residual_sum + moe_sum).astype(jnp.bfloat16)
```

```python
import functools
import math

import jax
import jax.numpy as jnp
from jax import lax
from jax.experimental import pallas as pl
from jax.experimental.pallas import tpu as pltpu
from jax.sharding import PartitionSpec as P

NOPE = 128
ROPE = 64
F32 = jnp.float32
BF16 = jnp.bfloat16
PASS_ROWS = 256


def repeat(count, step):
    if count <= 15:
        for i in range(count):
            step(i)
    else:
        lax.fori_loop(0, count, lambda i, carry: (step(i), carry)[1], 0)


def layer_kernel(
    C, X, H,
    lat_ref, q_ref, wuk_ref, wuv_ref, wo_ref, resid_ref, gain_ref, wg_ref, wu_ref, wd_ref,
    ids_ref, rw_ref,
    out_ref,
    lat_all, q_all, wuk, wuv, wo, wg, wu, wd, k_all, v_all, att, part, s2, r2, rs_all, xg, hg,
    xown, ob, rb,
    wsem, lsem, s1s, s1r, s2s, s2r, s3zs, s3zr, s3xs, s3xr, s3hs, s3hr, s4s, s4r, s5s, s5r,
):
    EH = X * H
    n = C * EH
    c, x, h = lax.axis_index("ctx"), lax.axis_index("exp"), lax.axis_index("head")
    e = x * H + h
    me = c * EH + e
    qb = lat_ref.shape[0]
    R = C * qb
    latent_width = wuk_ref.shape[0]
    head_width = NOPE + ROPE
    heads = q_ref.shape[1] // head_width
    tok = ids_ref.shape[1]
    cols = wo_ref.shape[1]
    ff = wg_ref.shape[2]
    aligned = cols % 128 == 0

    def device(cc, ee):
        return {"ctx": cc, "exp": ee // H, "head": lax.rem(ee, H)}

    def remote(src, dst, send, recv, cc, ee):
        return pltpu.make_async_remote_copy(
            src_ref=src, dst_ref=dst, send_sem=send, recv_sem=recv,
            device_id=device(cc, ee), device_id_type=pl.DeviceIdType.MESH)

    def peer(d):
        p = lax.rem(me + d, n)
        return p // EH, lax.rem(p, EH)

    def resid_piece(cc):
        if aligned:
            return resid_ref.at[:, pl.ds(pl.multiple_of(cc * cols, 128), cols)]
        return resid_ref.at[cc]

    barrier = pltpu.get_barrier_semaphore()

    def greet(i):
        pc, pe = peer(i + 1)
        pl.semaphore_signal(barrier, inc=1, device_id=device(pc, pe),
                            device_id_type=pl.DeviceIdType.MESH)

    repeat(n - 1, greet)
    loads = [
        pltpu.make_async_copy(lat_ref, lat_all.at[c], lsem.at[0]),
        pltpu.make_async_copy(q_ref, q_all.at[c], lsem.at[1]),
        pltpu.make_async_copy(resid_piece(c), rs_all.at[c], lsem.at[2]),
    ]
    weights = [
        pltpu.make_async_copy(wuk_ref, wuk, wsem.at[0]),
        pltpu.make_async_copy(wuv_ref, wuv, wsem.at[1]),
        pltpu.make_async_copy(wo_ref, wo, wsem.at[2]),
        pltpu.make_async_copy(wg_ref.at[0], wg, wsem.at[3]),
        pltpu.make_async_copy(wu_ref.at[0], wu, wsem.at[4]),
        pltpu.make_async_copy(wd_ref.at[0], wd, wsem.at[5]),
    ]
    for copy in loads + weights:
        copy.start()
    pl.semaphore_wait(barrier, n - 1)

    def s1(d, which, back):
        s, t = lax.rem(c + C - d, C), lax.rem(c + d, C)
        buf = [lat_all, q_all, rs_all][which]
        src = buf.at[s] if back else [lat_ref, q_ref, resid_piece(t)][which]
        dst = buf.at[s if back else c]
        return remote(src, dst, s1s.at[which, d - 1], s1r.at[which, d - 1], t, e)

    for which in range(3):
        for d in range(1, C):
            s1(d, which, False).start()
    for copy in loads:
        copy.wait()
    for which in range(2):
        for d in range(1, C):
            s1(d, which, True).wait_recv()

    weights[0].wait()
    weights[1].wait()
    G1 = C if R <= PASS_ROWS else 1

    def project(i):
        rows = lat_all[pl.ds(i * G1, G1), :, :latent_width].reshape(G1 * qb, latent_width)
        at = pl.ds(i * G1 * qb, G1 * qb)
        k_all[at, :] = jnp.dot(rows, wuk[...], preferred_element_type=F32).astype(BF16)
        v_all[at, :] = jnp.dot(rows, wuv[...], preferred_element_type=F32).astype(BF16)

    repeat(C // G1, project)
    weights[2].wait()
    scale = 1.0 / math.sqrt(head_width)

    def attend(i):
        qrows = q_all[pl.ds(i * G1, G1)].reshape(G1 * qb, q_ref.shape[1])
        rope_keys = lat_all[:, :, latent_width:].reshape(R, ROPE)
        qpos = i * G1 * qb + lax.broadcasted_iota(jnp.int32, (G1 * qb, R), 0)
        allowed = lax.broadcasted_iota(jnp.int32, (G1 * qb, R), 1) <= qpos
        at = pl.ds(i * G1 * qb, G1 * qb)
        nt = (((1,), (1,)), ((), ()))
        for head in range(heads):
            q = qrows[:, head * head_width:(head + 1) * head_width]
            span = slice(head * NOPE, (head + 1) * NOPE)
            scores = lax.dot_general(q[:, :NOPE], k_all[:, span], nt, preferred_element_type=F32)
            scores += lax.dot_general(q[:, NOPE:], rope_keys, nt, preferred_element_type=F32)
            scores = jnp.where(allowed, scores * scale, -1e30)
            exponent = jnp.where(
                allowed, jnp.exp(scores - jnp.max(scores, axis=1, keepdims=True)), 0.0)
            total = jnp.sum(exponent, axis=1, keepdims=True)
            mixed = jnp.dot(exponent.astype(BF16), v_all[:, span], preferred_element_type=F32)
            att[at, span] = (mixed / total).astype(BF16)
        part[at, :] = jnp.dot(att[at, :], wo[...], preferred_element_type=F32)

    repeat(C // G1, attend)

    for ee in range(EH):
        s2[ee] = jnp.concatenate(
            [part[cc * qb + ee * tok:cc * qb + (ee + 1) * tok, :] for cc in range(C)],
            axis=0).astype(BF16)

    def s2copy(d):
        te = lax.rem(e + d, EH)
        return remote(s2.at[te], r2.at[d - 1], s2s.at[d - 1], s2r.at[d - 1], c, te)

    for d in range(EH - 1, 0, -1):
        s2copy(d).start()
    for d in range(1, C):
        s1(d, 2, True).wait_recv()
    mine = jnp.concatenate([rs_all[cc].astype(F32) for cc in range(C)], axis=0)
    mine += s2[e].astype(F32)
    for d in range(1, EH):
        s2copy(d).wait_recv()
        mine += r2[d - 1].astype(F32)
    xg[c, e] = mine.astype(BF16)

    def block(dc, dx, dh):
        xe = lax.rem(x + X - dx, X) * H + lax.rem(h + H - dh, H)
        return xg.at[lax.rem(c + C - dc, C), xe]

    def zcopy(d, back):
        ref = block(d if back else 0, 0, 0)
        return remote(ref, ref, s3zs.at[d - 1], s3zr.at[d - 1], lax.rem(c + d, C), e)

    def xcopy(dc, dx, back):
        ref = block(dc, dx if back else 0, 0)
        return remote(ref, ref, s3xs.at[dc, dx - 1], s3xr.at[dc, dx - 1], c,
                      lax.rem(x + dx, X) * H + h)

    def hcopy(dc, dx, dh, back):
        ref = block(dc, dx, dh if back else 0)
        return remote(ref, ref, s3hs.at[dc, dx, dh - 1], s3hr.at[dc, dx, dh - 1], c,
                      x * H + lax.rem(h + dh, H))

    for d in range(C - 1, 0, -1):
        zcopy(d, False).start()

    def pass_on(dc):
        if not (isinstance(dc, int) and dc == 0):
            zcopy(dc, True).wait_recv()
        for dx in range(1, X):
            xcopy(dc, dx, False).start()
        for dh in range(1, H):
            hcopy(dc, 0, dh, False).start()

    def pass_head(dc):
        for dx in range(1, X):
            xcopy(dc, dx, True).wait_recv()
            for dh in range(1, H):
                hcopy(dc, dx, dh, False).start()

    chunk_rows = H * C * tok

    def gain_piece(cc):
        if aligned:
            return gain_ref[...].reshape(1, C * cols)[:, cc * cols:(cc + 1) * cols]
        return gain_ref[cc]

    def chunk_of(dx):
        return lax.rem(x + X - dx, X)

    def hidden(dx):
        first = chunk_of(dx) * H

        def rows_of(cc):
            return xg[cc, pl.ds(first, H)].reshape(chunk_rows, cols).astype(F32)

        square = jnp.zeros((chunk_rows, 1), F32)
        for cc in range(C):
            v = rows_of(cc)
            square += jnp.sum(v * v, axis=1, keepdims=True)
        inverse = lax.rsqrt(square / (C * cols) + 1e-6)
        gate = jnp.zeros((chunk_rows, ff), F32)
        up = jnp.zeros((chunk_rows, ff), F32)
        for cc in range(C):
            normed = (rows_of(cc) * inverse * gain_piece(cc)).astype(BF16)
            span = slice(cc * cols, (cc + 1) * cols)
            gate += jnp.dot(normed, wg[span, :], preferred_element_type=F32)
            up += jnp.dot(normed, wu[span, :], preferred_element_type=F32)
        hg[c, chunk_of(dx)] = (gate / (1.0 + jnp.exp(-gate)) * up).astype(BF16)

    def s4(dx, k, way, back):
        b = c - way * (k + 1 if back else k)
        ref = hg.at[jnp.clip(b, 0, C - 1), chunk_of(dx)]
        side = 0 if way > 0 else 1
        return remote(ref, ref, s4s.at[side, dx, k], s4r.at[side, dx, k],
                      jnp.clip(c + way, 0, C - 1), e)

    def inside(b):
        return jnp.logical_and(b >= 0, b < C)

    def s4_pass(dx, k):
        for way in (1, -1):
            if k > 0:
                @pl.when(inside(c - way * k))
                def _():
                    s4(dx, k - 1, way, True).wait_recv()
            if k < C - 1:
                @pl.when(jnp.logical_and(inside(c - way * k), inside(c + way)))
                def _():
                    s4(dx, k, way, False).start()

    def down(dx):
        total = jnp.zeros((chunk_rows, cols), F32)
        for cc in range(C):
            total += jnp.dot(hg[cc, chunk_of(dx)], wd[cc * ff:(cc + 1) * ff, :],
                             preferred_element_type=F32)
        ob[pl.ds(chunk_of(dx) * H * C, H * C)] = total.reshape(H * C, tok, cols).astype(BF16)

    def s5(dc, dx, dh, back):
        pc, pe = lax.rem(c + dc, C), chunk_of(dx) * H + lax.rem(h + dh, H)
        src = ob.at[pe * C + pc]
        if back:
            dst = rb.at[lax.rem(c + C - dc, C), lax.rem(x + dx, X) * H + lax.rem(h + H - dh, H)]
        else:
            dst = rb.at[c, e]
        return remote(src, dst, s5s.at[dc, dx, dh], s5r.at[dc, dx, dh], pc, pe)

    def s5_each(dx, act):
        for dh in range(H):
            skip = 1 if dx == 0 and dh == 0 else 0
            repeat(C - skip, lambda i: act(s5(C - 1 - i, dx, dh, False)))

    def s5_arrived(dx):
        for dh in range(H):
            skip = 1 if dx == 0 and dh == 0 else 0
            repeat(C - skip, lambda i: s5(C - 1 - i, dx, dh, True).wait_recv())

    for dc in range(C):
        pass_on(dc)
    for dc in range(C):
        for dh in range(1, H):
            hcopy(dc, 0, dh, True).wait_recv()
    weights[3].wait()
    weights[4].wait()
    hidden(0)
    s4_pass(0, 0)
    for dc in range(C):
        pass_head(dc)
    for cc in range(C):
        xown[cc] = xg[cc, e].astype(F32)
    for dx in range(1, X):
        for dc in range(C):
            for dh in range(1, H):
                hcopy(dc, dx, dh, True).wait_recv()
        hidden(dx)
        s4_pass(dx, 0)
    for k in range(1, C - 1):
        for dx in range(X):
            s4_pass(dx, k)
    weights[5].wait()
    for dx in range(X):
        s4_pass(dx, C - 1)
        down(dx)
        s5_each(dx, lambda copy: copy.start())
    rb[c, e] = ob[e * C + c]
    for dx in range(X):
        s5_arrived(dx)
    ids = ids_ref[...]
    rw = rw_ref[...]
    corner = (tok, tok)
    diagonal = (lax.broadcasted_iota(jnp.int32, corner, 0)
                == lax.broadcasted_iota(jnp.int32, corner, 1))
    picks = []
    for ee in range(EH):
        row = jnp.sum(jnp.where(ids == ee, rw, 0.0), axis=0, keepdims=True)
        picks.append(jnp.sum(jnp.where(diagonal, row, 0.0), axis=1, keepdims=True))
    for cc in range(C):
        total = xown[cc, pl.ds(pl.multiple_of(c * tok, tok), tok), :]
        for ee in range(EH):
            total += picks[ee] * rb[cc, ee].astype(F32)
        if aligned:
            out_ref[:, cc * cols:(cc + 1) * cols] = total.astype(BF16)
        else:
            out_ref[cc] = total.astype(BF16)

    for which in range(3):
        for d in range(1, C):
            s1(d, which, False).wait_send()
    for d in range(1, EH):
        s2copy(d).wait_send()
    for d in range(1, C):
        zcopy(d, False).wait_send()
    for dc in range(C):
        for dx in range(1, X):
            xcopy(dc, dx, False).wait_send()
        for dx in range(X):
            for dh in range(1, H):
                hcopy(dc, dx, dh, False).wait_send()
    for dx in range(X):
        s5_each(dx, lambda copy: copy.wait_send())
        for k in range(C - 1):
            for way in (1, -1):
                @pl.when(jnp.logical_and(inside(c - way * k), inside(c + way)))
                def _():
                    s4(dx, k, way, False).wait_send()


def shards(latent, query, w_uk, w_uv, w_o, resid, norm_gain, w_gate, w_up, w_down,
           expert_ids, route_weights):
    C, X, H = (lax.axis_size(a) for a in ("ctx", "exp", "head"))
    EH = X * H
    n = C * EH
    qb = latent.shape[0]
    R = C * qb
    tok, D = resid.shape
    cols = w_o.shape[1]
    ff = w_gate.shape[2]
    aligned = cols % 128 == 0
    if aligned:
        out_shape = (tok, D)
        resid_in, gain_in = resid, norm_gain
    else:
        out_shape = (C, tok, cols)
        resid_in = resid.reshape(tok, C, cols).transpose(1, 0, 2)
        gain_in = norm_gain.reshape(C, 1, cols)
    rows = C * tok
    dma = pltpu.SemaphoreType.DMA
    far = pl.BlockSpec(memory_space=pl.ANY)
    near = pl.BlockSpec(memory_space=pltpu.VMEM)
    out = pl.pallas_call(
        functools.partial(layer_kernel, C, X, H),
        out_shape=jax.ShapeDtypeStruct(out_shape, BF16),
        in_specs=[far, far, far, far, far, far, near, far, far, far, near, near],
        out_specs=near,
        scratch_shapes=[
            pltpu.VMEM((C,) + latent.shape, BF16),
            pltpu.VMEM((C,) + query.shape, BF16),
            pltpu.VMEM(w_uk.shape, BF16),
            pltpu.VMEM(w_uv.shape, BF16),
            pltpu.VMEM(w_o.shape, BF16),
            pltpu.VMEM(w_gate.shape[1:], BF16),
            pltpu.VMEM(w_up.shape[1:], BF16),
            pltpu.VMEM(w_down.shape[1:], BF16),
            pltpu.VMEM((R, w_uk.shape[1]), BF16),
            pltpu.VMEM((R, w_uv.shape[1]), BF16),
            pltpu.VMEM((R, w_uv.shape[1]), BF16),
            pltpu.VMEM((R, cols), F32),
            pltpu.VMEM((EH, rows, cols), BF16),
            pltpu.VMEM((EH - 1, rows, cols), BF16),
            pltpu.VMEM((C, tok, cols), BF16),
            pltpu.VMEM((C, EH, rows, cols), BF16),
            pltpu.VMEM((C, X, H * rows, ff), BF16),
            pltpu.VMEM((C, rows, cols), F32),
            pltpu.VMEM((n, tok, cols), BF16),
            pltpu.VMEM((C, EH, tok, cols), BF16),
            dma((6,)), dma((3,)),
            dma((3, C - 1)), dma((3, C - 1)),
            dma((EH - 1,)), dma((EH - 1,)),
            dma((C - 1,)), dma((C - 1,)),
            dma((C, X - 1)), dma((C, X - 1)),
            dma((C, X, H - 1)), dma((C, X, H - 1)),
            dma((2, X, C - 1)), dma((2, X, C - 1)),
            dma((C, X, H)), dma((C, X, H)),
        ],
        compiler_params=pltpu.CompilerParams(
            collective_id=0, has_side_effects=True, vmem_limit_bytes=60000 * 1024),
        name="layer",
    )(latent, query, w_uk, w_uv, w_o, resid_in, gain_in, w_gate, w_up, w_down,
      expert_ids.T, route_weights.T)
    return out if aligned else out.transpose(1, 0, 2).reshape(tok, D)


def solution(mesh):
    placed = (
        P(("groups", "ctx"), None),
        P(("groups", "ctx"), ("exp", "head")),
        P(None, ("exp", "head")),
        P(None, ("exp", "head")),
        P(("exp", "head"), "ctx"),
        P(("groups", "ctx", "exp", "head"), None),
        P(),
        P(("exp", "head"), None, "ctx"),
        P(("exp", "head"), None, "ctx"),
        P(("exp", "head"), None, "ctx"),
        P(("groups", "ctx", "exp", "head"), None),
        P(("groups", "ctx", "exp", "head"), None),
    )
    return jax.shard_map(
        shards,
        mesh=mesh,
        in_specs=placed,
        out_specs=P(("groups", "ctx", "exp", "head"), None),
        check_vma=False,
    )
```

```python
import functools
import math

import jax
import jax.numpy as jnp
from jax import lax
from jax.experimental import pallas as pl
from jax.experimental.pallas import tpu as pltpu
from jax.sharding import PartitionSpec as P

NOPE = 128
ROPE = 64
F32 = jnp.float32
BF16 = jnp.bfloat16
PASS_ROWS = 256


def repeat(count, step):
    if count <= 15:
        for i in range(count):
            step(i)
    else:
        lax.fori_loop(0, count, lambda i, carry: (step(i), carry)[1], 0)


def layer_kernel(
    C, X, H,
    lat_ref, q_ref, wuk_ref, wuv_ref, wo_ref, resid_ref, gain_ref, wg_ref, wu_ref, wd_ref,
    ids_ref, rw_ref,
    out_ref,
    lat_all, q_all, wuk, wuv, wo, wg, wu, wd, k_all, v_all, att, part, s2, r2, rs_all, xg, hg,
    xown, ob, rb,
    wsem, lsem, s1s, s1r, s2s, s2r, s3zs, s3zr, s3xs, s3xr, s3hs, s3hr, s4s, s4r, s5s, s5r,
):
    EH = X * H
    n = C * EH
    c, x, h = lax.axis_index("ctx"), lax.axis_index("exp"), lax.axis_index("head")
    e = x * H + h
    me = c * EH + e
    qb = lat_ref.shape[0]
    R = C * qb
    latent_width = wuk_ref.shape[0]
    head_width = NOPE + ROPE
    heads = q_ref.shape[1] // head_width
    tok = ids_ref.shape[1]
    cols = wo_ref.shape[1]
    ff = wg_ref.shape[2]
    aligned = cols % 128 == 0

    def device(cc, ee):
        return {"ctx": cc, "exp": ee // H, "head": lax.rem(ee, H)}

    def remote(src, dst, send, recv, cc, ee):
        return pltpu.make_async_remote_copy(
            src_ref=src, dst_ref=dst, send_sem=send, recv_sem=recv,
            device_id=device(cc, ee), device_id_type=pl.DeviceIdType.MESH)

    def peer(d):
        p = lax.rem(me + d, n)
        return p // EH, lax.rem(p, EH)

    def resid_piece(cc):
        if aligned:
            return resid_ref.at[:, pl.ds(pl.multiple_of(cc * cols, 128), cols)]
        return resid_ref.at[cc]

    barrier = pltpu.get_barrier_semaphore()

    def greet(i):
        pc, pe = peer(i + 1)
        pl.semaphore_signal(barrier, inc=1, device_id=device(pc, pe),
                            device_id_type=pl.DeviceIdType.MESH)

    repeat(n - 1, greet)
    loads = [
        pltpu.make_async_copy(lat_ref, lat_all.at[c], lsem.at[0]),
        pltpu.make_async_copy(q_ref, q_all.at[c], lsem.at[1]),
        pltpu.make_async_copy(resid_piece(c), rs_all.at[c], lsem.at[2]),
    ]
    weights = [
        pltpu.make_async_copy(wuk_ref, wuk, wsem.at[0]),
        pltpu.make_async_copy(wuv_ref, wuv, wsem.at[1]),
        pltpu.make_async_copy(wo_ref, wo, wsem.at[2]),
        pltpu.make_async_copy(wg_ref.at[0], wg, wsem.at[3]),
        pltpu.make_async_copy(wu_ref.at[0], wu, wsem.at[4]),
        pltpu.make_async_copy(wd_ref.at[0], wd, wsem.at[5]),
    ]
    for copy in loads + weights:
        copy.start()
    pl.semaphore_wait(barrier, n - 1)

    def s1(d, which, back):
        s, t = lax.rem(c + C - d, C), lax.rem(c + d, C)
        buf = [lat_all, q_all, rs_all][which]
        src = buf.at[s] if back else [lat_ref, q_ref, resid_piece(t)][which]
        dst = buf.at[s if back else c]
        return remote(src, dst, s1s.at[which, d - 1], s1r.at[which, d - 1], t, e)

    for which in range(2):
        for d in range(C - 1, 0, -1):
            s1(d, which, False).start()
    for copy in loads:
        copy.wait()
    for d in range(1, C):
        s1(d, 0, True).wait_recv()

    weights[0].wait()
    weights[1].wait()
    G1 = C if R <= PASS_ROWS else 1

    def project(i):
        rows = lat_all[pl.ds(i * G1, G1), :, :latent_width].reshape(G1 * qb, latent_width)
        at = pl.ds(i * G1 * qb, G1 * qb)
        k_all[at, :] = jnp.dot(rows, wuk[...], preferred_element_type=F32).astype(BF16)
        v_all[at, :] = jnp.dot(rows, wuv[...], preferred_element_type=F32).astype(BF16)

    repeat(C // G1, project)
    for d in range(1, C):
        s1(d, 1, True).wait_recv()
    for d in range(C - 1, 0, -1):
        s1(d, 2, False).start()
    weights[2].wait()
    scale = 1.0 / math.sqrt(head_width)

    def attend(i):
        qrows = q_all[pl.ds(i * G1, G1)].reshape(G1 * qb, q_ref.shape[1])
        rope_keys = lat_all[:, :, latent_width:].reshape(R, ROPE)
        qpos = i * G1 * qb + lax.broadcasted_iota(jnp.int32, (G1 * qb, R), 0)
        allowed = lax.broadcasted_iota(jnp.int32, (G1 * qb, R), 1) <= qpos
        at = pl.ds(i * G1 * qb, G1 * qb)
        nt = (((1,), (1,)), ((), ()))
        for head in range(heads):
            q = qrows[:, head * head_width:(head + 1) * head_width]
            span = slice(head * NOPE, (head + 1) * NOPE)
            scores = lax.dot_general(q[:, :NOPE], k_all[:, span], nt, preferred_element_type=F32)
            scores += lax.dot_general(q[:, NOPE:], rope_keys, nt, preferred_element_type=F32)
            scores = jnp.where(allowed, scores * scale, -1e30)
            exponent = jnp.where(
                allowed, jnp.exp(scores - jnp.max(scores, axis=1, keepdims=True)), 0.0)
            total = jnp.sum(exponent, axis=1, keepdims=True)
            mixed = jnp.dot(exponent.astype(BF16), v_all[:, span], preferred_element_type=F32)
            att[at, span] = (mixed / total).astype(BF16)
        part[at, :] = jnp.dot(att[at, :], wo[...], preferred_element_type=F32)

    repeat(C // G1, attend)

    for ee in range(EH):
        s2[ee] = jnp.concatenate(
            [part[cc * qb + ee * tok:cc * qb + (ee + 1) * tok, :] for cc in range(C)],
            axis=0).astype(BF16)

    def s2copy(d):
        te = lax.rem(e + d, EH)
        return remote(s2.at[te], r2.at[d - 1], s2s.at[d - 1], s2r.at[d - 1], c, te)

    for d in range(EH - 1, 0, -1):
        s2copy(d).start()
    for d in range(1, C):
        s1(d, 2, True).wait_recv()
    mine = jnp.concatenate([rs_all[cc].astype(F32) for cc in range(C)], axis=0)
    mine += s2[e].astype(F32)
    for d in range(1, EH):
        s2copy(d).wait_recv()
        mine += r2[d - 1].astype(F32)
    xg[c, e] = mine.astype(BF16)

    def block(dc, dx, dh):
        xe = lax.rem(x + X - dx, X) * H + lax.rem(h + H - dh, H)
        return xg.at[lax.rem(c + C - dc, C), xe]

    def zcopy(d, back):
        ref = block(d if back else 0, 0, 0)
        return remote(ref, ref, s3zs.at[d - 1], s3zr.at[d - 1], lax.rem(c + d, C), e)

    def xcopy(dc, dx, back):
        ref = block(dc, dx if back else 0, 0)
        return remote(ref, ref, s3xs.at[dc, dx - 1], s3xr.at[dc, dx - 1], c,
                      lax.rem(x + dx, X) * H + h)

    def hcopy(dc, dx, dh, back):
        ref = block(dc, dx, dh if back else 0)
        return remote(ref, ref, s3hs.at[dc, dx, dh - 1], s3hr.at[dc, dx, dh - 1], c,
                      x * H + lax.rem(h + dh, H))

    for d in range(C - 1, 0, -1):
        zcopy(d, False).start()

    def pass_on(dc):
        if not (isinstance(dc, int) and dc == 0):
            zcopy(dc, True).wait_recv()
        for dx in range(1, X):
            xcopy(dc, dx, False).start()
        for dh in range(1, H):
            hcopy(dc, 0, dh, False).start()

    def pass_head(dc):
        for dx in range(1, X):
            xcopy(dc, dx, True).wait_recv()
            for dh in range(1, H):
                hcopy(dc, dx, dh, False).start()

    chunk_rows = H * C * tok

    def gain_piece(cc):
        if aligned:
            return gain_ref[...].reshape(1, C * cols)[:, cc * cols:(cc + 1) * cols]
        return gain_ref[cc]

    def chunk_of(dx):
        return lax.rem(x + X - dx, X)

    def hidden(dx):
        first = chunk_of(dx) * H

        def rows_of(cc):
            return xg[cc, pl.ds(first, H)].reshape(chunk_rows, cols).astype(F32)

        square = jnp.zeros((chunk_rows, 1), F32)
        for cc in range(C):
            v = rows_of(cc)
            square += jnp.sum(v * v, axis=1, keepdims=True)
        inverse = lax.rsqrt(square / (C * cols) + 1e-6)
        gate = jnp.zeros((chunk_rows, ff), F32)
        up = jnp.zeros((chunk_rows, ff), F32)
        for cc in range(C):
            normed = (rows_of(cc) * inverse * gain_piece(cc)).astype(BF16)
            span = slice(cc * cols, (cc + 1) * cols)
            gate += jnp.dot(normed, wg[span, :], preferred_element_type=F32)
            up += jnp.dot(normed, wu[span, :], preferred_element_type=F32)
        hg[c, chunk_of(dx)] = (gate / (1.0 + jnp.exp(-gate)) * up).astype(BF16)

    def s4(dx, k, way, back):
        b = c - way * (k + 1 if back else k)
        ref = hg.at[jnp.clip(b, 0, C - 1), chunk_of(dx)]
        side = 0 if way > 0 else 1
        return remote(ref, ref, s4s.at[side, dx, k], s4r.at[side, dx, k],
                      jnp.clip(c + way, 0, C - 1), e)

    def inside(b):
        return jnp.logical_and(b >= 0, b < C)

    def s4_pass(dx, k):
        for way in (1, -1):
            if k > 0:
                @pl.when(inside(c - way * k))
                def _():
                    s4(dx, k - 1, way, True).wait_recv()
            if k < C - 1:
                @pl.when(jnp.logical_and(inside(c - way * k), inside(c + way)))
                def _():
                    s4(dx, k, way, False).start()

    def down(dx):
        total = jnp.zeros((chunk_rows, cols), F32)
        for cc in range(C):
            total += jnp.dot(hg[cc, chunk_of(dx)], wd[cc * ff:(cc + 1) * ff, :],
                             preferred_element_type=F32)
        ob[pl.ds(chunk_of(dx) * H * C, H * C)] = total.reshape(H * C, tok, cols).astype(BF16)

    def s5(dc, dx, dh, back):
        pc, pe = lax.rem(c + dc, C), chunk_of(dx) * H + lax.rem(h + dh, H)
        src = ob.at[pe * C + pc]
        if back:
            dst = rb.at[lax.rem(c + C - dc, C), lax.rem(x + dx, X) * H + lax.rem(h + H - dh, H)]
        else:
            dst = rb.at[c, e]
        return remote(src, dst, s5s.at[dc, dx, dh], s5r.at[dc, dx, dh], pc, pe)

    def s5_each(dx, act):
        for dh in range(H):
            skip = 1 if dx == 0 and dh == 0 else 0
            repeat(C - skip, lambda i: act(s5(C - 1 - i, dx, dh, False)))

    def s5_arrived(dx):
        for dh in range(H):
            skip = 1 if dx == 0 and dh == 0 else 0
            repeat(C - skip, lambda i: s5(C - 1 - i, dx, dh, True).wait_recv())

    for dc in range(C):
        pass_on(dc)
    for dc in range(C):
        for dh in range(1, H):
            hcopy(dc, 0, dh, True).wait_recv()
    weights[3].wait()
    weights[4].wait()
    hidden(0)
    s4_pass(0, 0)
    for dc in range(C):
        pass_head(dc)
    for cc in range(C):
        xown[cc] = xg[cc, e].astype(F32)
    for dx in range(1, X):
        for dc in range(C):
            for dh in range(1, H):
                hcopy(dc, dx, dh, True).wait_recv()
        hidden(dx)
        s4_pass(dx, 0)
    for k in range(1, C - 1):
        for dx in range(X):
            s4_pass(dx, k)
    weights[5].wait()
    for dx in range(X):
        s4_pass(dx, C - 1)
        down(dx)
        s5_each(dx, lambda copy: copy.start())
    rb[c, e] = ob[e * C + c]
    for dx in range(X):
        s5_arrived(dx)
    ids = ids_ref[...]
    rw = rw_ref[...]
    corner = (tok, tok)
    diagonal = (lax.broadcasted_iota(jnp.int32, corner, 0)
                == lax.broadcasted_iota(jnp.int32, corner, 1))
    picks = []
    for ee in range(EH):
        row = jnp.sum(jnp.where(ids == ee, rw, 0.0), axis=0, keepdims=True)
        picks.append(jnp.sum(jnp.where(diagonal, row, 0.0), axis=1, keepdims=True))
    for cc in range(C):
        total = xown[cc, pl.ds(pl.multiple_of(c * tok, tok), tok), :]
        for ee in range(EH):
            total += picks[ee] * rb[cc, ee].astype(F32)
        if aligned:
            out_ref[:, cc * cols:(cc + 1) * cols] = total.astype(BF16)
        else:
            out_ref[cc] = total.astype(BF16)

    for which in range(3):
        for d in range(1, C):
            s1(d, which, False).wait_send()
    for d in range(1, EH):
        s2copy(d).wait_send()
    for d in range(1, C):
        zcopy(d, False).wait_send()
    for dc in range(C):
        for dx in range(1, X):
            xcopy(dc, dx, False).wait_send()
        for dx in range(X):
            for dh in range(1, H):
                hcopy(dc, dx, dh, False).wait_send()
    for dx in range(X):
        s5_each(dx, lambda copy: copy.wait_send())
        for k in range(C - 1):
            for way in (1, -1):
                @pl.when(jnp.logical_and(inside(c - way * k), inside(c + way)))
                def _():
                    s4(dx, k, way, False).wait_send()


def shards(latent, query, w_uk, w_uv, w_o, resid, norm_gain, w_gate, w_up, w_down,
           expert_ids, route_weights):
    C, X, H = (lax.axis_size(a) for a in ("ctx", "exp", "head"))
    EH = X * H
    n = C * EH
    qb = latent.shape[0]
    R = C * qb
    tok, D = resid.shape
    cols = w_o.shape[1]
    ff = w_gate.shape[2]
    aligned = cols % 128 == 0
    if aligned:
        out_shape = (tok, D)
        resid_in, gain_in = resid, norm_gain
    else:
        out_shape = (C, tok, cols)
        resid_in = resid.reshape(tok, C, cols).transpose(1, 0, 2)
        gain_in = norm_gain.reshape(C, 1, cols)
    rows = C * tok
    dma = pltpu.SemaphoreType.DMA
    far = pl.BlockSpec(memory_space=pl.ANY)
    near = pl.BlockSpec(memory_space=pltpu.VMEM)
    out = pl.pallas_call(
        functools.partial(layer_kernel, C, X, H),
        out_shape=jax.ShapeDtypeStruct(out_shape, BF16),
        in_specs=[far, far, far, far, far, far, near, far, far, far, near, near],
        out_specs=near,
        scratch_shapes=[
            pltpu.VMEM((C,) + latent.shape, BF16),
            pltpu.VMEM((C,) + query.shape, BF16),
            pltpu.VMEM(w_uk.shape, BF16),
            pltpu.VMEM(w_uv.shape, BF16),
            pltpu.VMEM(w_o.shape, BF16),
            pltpu.VMEM(w_gate.shape[1:], BF16),
            pltpu.VMEM(w_up.shape[1:], BF16),
            pltpu.VMEM(w_down.shape[1:], BF16),
            pltpu.VMEM((R, w_uk.shape[1]), BF16),
            pltpu.VMEM((R, w_uv.shape[1]), BF16),
            pltpu.VMEM((R, w_uv.shape[1]), BF16),
            pltpu.VMEM((R, cols), F32),
            pltpu.VMEM((EH, rows, cols), BF16),
            pltpu.VMEM((EH - 1, rows, cols), BF16),
            pltpu.VMEM((C, tok, cols), BF16),
            pltpu.VMEM((C, EH, rows, cols), BF16),
            pltpu.VMEM((C, X, H * rows, ff), BF16),
            pltpu.VMEM((C, rows, cols), F32),
            pltpu.VMEM((n, tok, cols), BF16),
            pltpu.VMEM((C, EH, tok, cols), BF16),
            dma((6,)), dma((3,)),
            dma((3, C - 1)), dma((3, C - 1)),
            dma((EH - 1,)), dma((EH - 1,)),
            dma((C - 1,)), dma((C - 1,)),
            dma((C, X - 1)), dma((C, X - 1)),
            dma((C, X, H - 1)), dma((C, X, H - 1)),
            dma((2, X, C - 1)), dma((2, X, C - 1)),
            dma((C, X, H)), dma((C, X, H)),
        ],
        compiler_params=pltpu.CompilerParams(
            collective_id=0, has_side_effects=True, vmem_limit_bytes=60000 * 1024),
        name="layer",
    )(latent, query, w_uk, w_uv, w_o, resid_in, gain_in, w_gate, w_up, w_down,
      expert_ids.T, route_weights.T)
    return out if aligned else out.transpose(1, 0, 2).reshape(tok, D)


def solution(mesh):
    placed = (
        P(("groups", "ctx"), None),
        P(("groups", "ctx"), ("exp", "head")),
        P(None, ("exp", "head")),
        P(None, ("exp", "head")),
        P(("exp", "head"), "ctx"),
        P(("groups", "ctx", "exp", "head"), None),
        P(),
        P(("exp", "head"), None, "ctx"),
        P(("exp", "head"), None, "ctx"),
        P(("exp", "head"), None, "ctx"),
        P(("groups", "ctx", "exp", "head"), None),
        P(("groups", "ctx", "exp", "head"), None),
    )
    return jax.shard_map(
        shards,
        mesh=mesh,
        in_specs=placed,
        out_specs=P(("groups", "ctx", "exp", "head"), None),
        check_vma=False,
    )
```
